256 devices in a mesh: vocab: 4 (over y), docs: 64 (over x, z, core).
Axes of the slice: x: 4, y: 4, z: 8, core: 2. Of those that a mesh axis runs over, the one named last changes fastest.
Arguments:
- hidden: bfloat16 [192, 256, 2048], P('docs', 'vocab'), may hold values from -6 to 6
- w_vocab: bfloat16 [16384, 2048], P(('vocab', 'docs')), may hold values from -0.125 to 0.125
- lengths: int32 [192], P('docs'), may hold values from 1 to 256, as said below
- query_terms: bfloat16 [8192, 16384], P('docs', 'vocab'), may hold values from -0.25 to 0.25
- tile_routes: int32 [64, 128, 4], P('docs', 'vocab'), may hold values from 0 to 63, all different within a row; in each aligned block of 32 rows (0 to 31, 32 to 63, ..., all dimensions but the last counted through in order) at most 4 rows name the same one
Outputs:
- doc_terms: bfloat16 [192, 16384], P('docs', 'vocab')
- scores: float32 [8192, 192], P('docs', 'vocab')
The draws below stay inside these ranges and needn't reach their ends.
Inputs may be any that keep to these rules, and one draw needn't show every extreme that they name: `lengths`: the last passage has 256 tokens. `tile_routes`: each row names 4 different query tiles; among the 32 rows of one device no query tile is named more than 4 times.
All inputs are finite; a program needn't handle non-finite values.
Results may differ from the reference program's by a relative error of at most 0.009.
Values may be sent and summed in bfloat16 or wider, within the bound.
No kernel may reach another device: no remote copies, remote signals or barrier semaphores. Data moves between devices by JAX's collectives and lax.ppermute only.
A program may use at most 384 MiB of HBM per device.

```python
import math
import jax
import jax.numpy as jnp
import numpy as np
from jax import lax

D = 2048
V = 16384
S = 256
TILE = 128
QT = 128
TOP = 4
P_DEV = 3
PASSAGES = 192
NQ = 8192
TT = 128
TT_DEV = 32
CAP = 4
N_DOCS = 64


def draw_hidden(key, part):
    key_common, key_noise = jax.random.split(jax.random.fold_in(key, 11), 2)
    common = jax.random.normal(key_common, (PASSAGES, 1, D), jnp.float32)
    noise = jax.random.normal(key_noise, (PASSAGES, S, D), jnp.float32)
    values = common + 0.7 * noise
    return jnp.clip(values, -6.0, 6.0).astype(jnp.bfloat16)


def draw_lengths(key, part):
    places = jnp.arange(PASSAGES, dtype=jnp.int32)
    lowest = max(S // 16, 1)
    upper_end = S // 4 + (S - S // 4) * places // max(PASSAGES - 1, 1)
    raw_bits = jax.random.randint(jax.random.fold_in(key, 23), (PASSAGES,), 0, 1 << 20, jnp.int32)
    drawn = lowest + raw_bits % (upper_end - lowest + 1)
    return jnp.where(places == PASSAGES - 1, S, drawn).astype(jnp.int32)


def block_scale(rng, shape, shards, smallest, high):
    factor_of = 1.0
    for axis_at, blocks in shards:
        steps = jax.random.uniform(jax.random.fold_in(jax.random.fold_in(rng, 6), axis_at), (blocks,), jnp.float32, smallest / len(shards), high / len(shards))
        factor_of = factor_of * jnp.repeat(jnp.exp(steps), shape[axis_at] // blocks).reshape((-1,) + (1,) * (len(shape) - 1 - axis_at))
    return factor_of


def assign_block(key, own, number, rows, amount, top, reach, lean):
    ranking = jax.random.permutation(key, amount)
    crowded, usual = shares(amount, rows * top, reach, lean, True), shares(amount, rows * top, reach, lean, False)
    places = jnp.arange(amount)

    def named(sizes, rotation):
        used = int((sizes > 0).sum())
        fixed = max(1, used // 4)
        moved = fixed + (places - fixed + rotation * (used - fixed)) % max(1, amount - fixed)
        return jnp.zeros((amount,), jnp.int32).at[ranking[jnp.where(places < fixed, places, moved)]].set(jnp.asarray(sizes, jnp.int32))

    sizes = jnp.where(number % 4 == 0, named(crowded, number // 4), named(usual, number - number // 4 - 1))
    mixed = jax.random.permutation(jax.random.fold_in(own, 3), amount)
    giver, taker = mixed[0:amount // 2 * 2:2], mixed[1:amount // 2 * 2:2]
    room = jnp.minimum(sizes[giver] - 1, reach - sizes[taker]) // 2
    room = jnp.where((giver == ranking[0]) | (taker == ranking[0]) | (sizes[taker] == 0), 0, jnp.maximum(room, 0))
    moved = jax.random.randint(jax.random.fold_in(own, 4), (amount // 2,), 0, 1 << 20) % (room + 1)
    sizes = sizes.at[giver].add(-moved).at[taker].add(moved)
    members = jnp.searchsorted(jnp.cumsum(sizes), jnp.arange(rows * top), side="right").astype(jnp.int32)
    listing = members.reshape(top, rows).T
    listing = listing[jax.random.permutation(jax.random.fold_in(own, 1), rows)]
    rotation = jax.random.randint(jax.random.fold_in(own, 2), (rows, 1), 0, top)
    return jnp.take_along_axis(listing, (jnp.arange(top)[None, :] + rotation) % top, axis=1)


def shares(number_of, total, limit, slope, full):
    weights = [(1 << 20) // math.isqrt(grade ** slope) + 1 for grade in range(1, number_of + 1)]
    largest = limit if full else min(limit, max(-(-total // number_of), total * weights[0] // sum(weights)))
    least = 1 if total - largest >= number_of - 1 else 0
    holding, rest = [largest] + [least] * (number_of - 1), total - largest - least * (number_of - 1)
    while rest > 0:
        candidates = [i for i in range(1, number_of) if holding[i] < largest] or [i for i in range(1, number_of) if holding[i] < limit]
        whole, budget = sum([weights[i] for i in candidates]), rest
        for i in candidates:
            extra = min(limit - holding[i], max(1, budget * weights[i] // whole), rest)
            holding[i] = holding[i] + extra
            rest = rest - extra
    return np.array(holding)


def centred(own_key, extent, spread, most, pieces=(), held_as=jnp.bfloat16):
    values = spread * jax.random.normal(own_key, extent, jnp.float32)
    if pieces:
        values = values * block_scale(own_key, extent, pieces, -0.22, 0.18)
    return jnp.clip(values, -most, most).astype(held_as)


def setup_inputs(seed: int = 0) -> dict:
    key_list = jax.random.split(jax.random.key(seed), 6)
    hidden = draw_hidden(jax.random.fold_in(key_list[5], 71), 0)
    w_vocab = centred(key_list[1], (V, D), D ** -0.5, 0.125, ((0, 256),))
    lengths = draw_lengths(jax.random.fold_in(key_list[5], 71), 0)
    query_terms = centred(key_list[3], (NQ, V), (0.6 * (TT * TOP * TILE // N_DOCS) ** -0.5), 0.25, ((0, 64), (1, 4)))
    tile_routes_keys = jax.random.split(jax.random.fold_in(key_list[4], 1), N_DOCS * TT // TT_DEV)
    tile_routes_turns = jax.random.permutation(jax.random.fold_in(key_list[4], 3), N_DOCS * TT // TT_DEV)
    tile_routes = jax.vmap(lambda own, number: assign_block(jax.random.fold_in(key_list[4], 2), own, number, TT_DEV, N_DOCS, TOP, CAP, 2))(tile_routes_keys, tile_routes_turns).reshape((N_DOCS, TT, TOP))
    return {"hidden": hidden, "w_vocab": w_vocab, "lengths": lengths, "query_terms": query_terms, "tile_routes": tile_routes}


saturate = 1.2
length_slope = 0.75


def reference(hidden, w_vocab, lengths, query_terms, tile_routes):
    lens_f = lengths.astype(jnp.float32)
    average = jnp.sum(lens_f) / PASSAGES

    def pool_one(inputs_pair):
        passage_rows, length_one = inputs_pair
        logits = jnp.dot(passage_rows, w_vocab.T, preferred_element_type=jnp.float32)
        valid_pos = jnp.arange(S, dtype=jnp.int32) < length_one
        activity = jnp.where(valid_pos[:, None], jnp.log1p(jnp.maximum(logits, 0.0)), 0.0)
        return jnp.sum(activity, axis=0) / length_one.astype(jnp.float32)

    pooled = lax.map(pool_one, (hidden, lengths))
    doc_terms = pooled.astype(jnp.bfloat16)
    weight = doc_terms.astype(jnp.float32)
    denominator = saturate * (1.0 - length_slope + length_slope * lens_f / average)
    scaled = (weight * (saturate + 1.0) / (weight + denominator[:, None])).astype(jnp.bfloat16)
    blocks = scaled.reshape(N_DOCS, P_DEV, TT, TILE)

    def score_tile(tile_index):
        listed = jnp.any(tile_routes == tile_index, axis=2)
        masked = (blocks * listed[:, None, :, None].astype(jnp.bfloat16)).reshape(PASSAGES, V)
        query_rows = lax.dynamic_slice_in_dim(query_terms, tile_index * QT, QT, 0)
        return lax.dot_general(query_rows, masked, (((1,), (1,)), ((), ())), preferred_element_type=jnp.float32)

    scores = lax.map(score_tile, jnp.arange(N_DOCS, dtype=jnp.int32)).reshape(NQ, PASSAGES)
    return doc_terms, scores
```

```python
import functools

import jax
import jax.numpy as jnp
from jax import lax
from jax.experimental import pallas as pl
from jax.experimental.pallas import tpu as pltpu
from jax.sharding import Mesh, PartitionSpec as P

saturate = 1.2
length_slope = 0.75
CORES = 2


def pool_kernel(block_count, passages, rows, chunk, valid_ref, *refs):
    blocks = refs[:block_count]
    w_ref, lens_ref, out_ref, held, sems = refs[block_count:]
    per = passages * rows

    @pl.when(pl.program_id(0) == 0)
    def _():
        copies = [
            pltpu.make_async_copy(blocks[b], held.at[pl.ds(b * per, per)], sems.at[b])
            for b in range(block_count)
        ]
        for copy in copies:
            copy.start()
        for copy in copies:
            copy.wait()

    owners = out_ref.shape[0] // passages
    weights = w_ref[...]
    row = lax.broadcasted_iota(jnp.int32, (8, weights.shape[0]), 0)
    sums = [None] * (owners * passages)
    for first in range(0, block_count, chunk):
        logits = lax.dot_general(
            held[first * per : (first + chunk) * per, :],
            weights,
            (((1,), (1,)), ((), ())),
            preferred_element_type=jnp.float32,
        )
        for b in range(first, first + chunk):
            for p in range(passages):
                valid = valid_ref[b * passages + p]
                grown = None
                for g in range(rows // 8):
                    at = (b - first) * per + p * rows + g * 8
                    x = jnp.where(row < valid - g * 8, jnp.maximum(logits[at : at + 8], 0.0), 0.0)
                    grown = x if grown is None else grown + (x + grown * x)
                shifted = 1.0 + grown
                small = shifted == 1.0
                ratio = grown / jnp.where(small, 1.0, shifted - 1.0)
                logs = jnp.where(small, grown, jnp.log(shifted) * ratio)
                slot = (b // (block_count // owners)) * passages + p
                sums[slot] = logs if sums[slot] is None else sums[slot] + logs
    pooled = jnp.concatenate([jnp.sum(s, axis=0, keepdims=True) for s in sums], axis=0)
    out_ref[...] = (pooled / lens_ref[:, :1]).astype(out_ref.dtype)


def pooled_terms(blocks, valid, lens, weights, tile=512, chunk=4):
    count = len(blocks)
    passages, rows, width = blocks[0].shape
    terms, lines = weights.shape[0], lens.shape[0]
    lens_f = jnp.broadcast_to(lens.astype(jnp.float32)[:, None], (lines, 128))
    return pl.pallas_call(
        functools.partial(pool_kernel, count, passages, rows, chunk),
        grid_spec=pltpu.PrefetchScalarGridSpec(
            num_scalar_prefetch=1,
            grid=(terms // tile,),
            in_specs=[pl.BlockSpec(memory_space=pl.ANY) for _ in blocks]
            + [
                pl.BlockSpec((tile, width), lambda i, v: (i, 0)),
                pl.BlockSpec((lines, 128), lambda i, v: (0, 0)),
            ],
            out_specs=pl.BlockSpec((lines, tile), lambda i, v: (0, i)),
            scratch_shapes=[
                pltpu.VMEM((count * passages * rows, width), jnp.bfloat16),
                pltpu.SemaphoreType.DMA((count,)),
            ],
        ),
        out_shape=jax.ShapeDtypeStruct((lines, terms), jnp.bfloat16),
        compiler_params=pltpu.CompilerParams(vmem_limit_bytes=56 << 20),
    )(valid, *[b.reshape(passages * rows, width) for b in blocks], weights, lens_f)


def steps(size, toward):
    return [
        (i * CORES + c, ((i + (toward if c == 0 else -toward)) % size) * CORES + c)
        for i in range(size)
        for c in range(CORES)
    ]


def swap_cores(a):
    return lax.ppermute(a, "c", [(0, 1), (1, 0)])


def local(hidden, w_vocab, lengths, query_terms, tile_routes):
    groups = lax.axis_size("y")
    members = lax.axis_size("x") * lax.axis_size("z") * CORES
    docs = ("x", "z", "c")
    local_count, rows, _ = hidden.shape
    y, core = lax.axis_index("y"), lax.axis_index("c")
    sign = 1 - 2 * core

    weights = lax.all_gather(w_vocab, ("x", "z"), axis=0, tiled=True)

    ahead = lax.ppermute(hidden, ("y", "c"), steps(groups, 1))
    behind = lax.ppermute(hidden, ("y", "c"), steps(groups, -1))
    across = lax.ppermute(ahead, ("y", "c"), steps(groups, 1))
    own = [hidden, ahead, behind, across]
    other = [swap_cores(a) for a in own]
    shifts = jnp.array([0, -1, 1, -2], jnp.int32)
    places = jnp.stack([(y + sign * shifts) % groups, (y - sign * shifts) % groups])
    lens_pair = jnp.stack([lengths, swap_cores(lengths)])
    valid = lens_pair[:, None, :] - places[:, :, None] * rows
    valid = jnp.clip(valid, 0, rows).reshape(-1)

    term_count = query_terms.shape[1]
    tile_count = term_count // 128
    my_routes = tile_routes[0]
    capacity = min(tile_count, 4)
    owners = lax.broadcasted_iota(jnp.int32, (1, 1, members), 2)
    is_listed = jnp.any(my_routes[:, :, None] == owners, axis=1)
    earlier = lax.broadcasted_iota(jnp.int32, (tile_count, tile_count), 0)
    later = lax.broadcasted_iota(jnp.int32, (tile_count, tile_count), 1)
    slot_index = (
        lax.dot_general(
            (earlier <= later).astype(jnp.bfloat16),
            is_listed.astype(jnp.bfloat16),
            (((0,), (0,)), ((), ())),
            preferred_element_type=jnp.float32,
        ).astype(jnp.int32)
        - 1
    )
    slot_ids = lax.broadcasted_iota(jnp.int32, (1, capacity, 1), 1)
    selector = (is_listed.T[:, None, :] & (slot_index.T[:, None, :] == slot_ids)).astype(
        jnp.bfloat16
    )
    tile_ids = lax.broadcasted_iota(jnp.float32, (1, 1, tile_count), 2)
    labels = jnp.sum(selector.astype(jnp.float32) * tile_ids, axis=2)
    lens_row = jnp.broadcast_to(lengths.astype(jnp.float32)[None], (members, local_count))
    notes = jnp.concatenate([labels, lens_row], axis=1).astype(jnp.bfloat16)
    notes_in = lax.all_to_all(notes, docs, split_axis=0, concat_axis=0, tiled=True)
    notes_in = notes_in.astype(jnp.float32)
    passage_total = members * local_count
    average = jnp.sum(notes_in[:, capacity:]) / passage_total
    placing = (notes_in[:, :capacity, None] == tile_ids).astype(jnp.bfloat16)
    denominator = saturate * (
        1.0 - length_slope + length_slope * lengths.astype(jnp.float32) / average
    )

    pooled = pooled_terms(own + other, valid, lens_pair.reshape(-1), weights)
    mine = pooled[:local_count].reshape(local_count, tile_count, 1, 64)
    theirs = swap_cores(pooled[local_count:]).reshape(local_count, tile_count, 1, 64)
    blocks = jnp.where(
        core == 0,
        jnp.concatenate([mine, theirs], axis=2),
        jnp.concatenate([theirs, mine], axis=2),
    ).reshape(local_count, tile_count, 128)
    doc_terms = blocks.reshape(local_count, term_count)

    weight = blocks.astype(jnp.float32)
    scaled = (weight * (saturate + 1.0) / (weight + denominator[:, None, None])).astype(
        jnp.bfloat16
    )
    outgoing = jnp.einsum(
        "oct,ptk->ocpk", selector, scaled, preferred_element_type=jnp.float32
    ).astype(jnp.bfloat16)
    arrived = lax.all_to_all(outgoing, docs, split_axis=0, concat_axis=0, tiled=True)
    masked = jnp.einsum(
        "bct,bcpk->bptk", placing, arrived, preferred_element_type=jnp.float32
    ).astype(jnp.bfloat16)
    masked = masked.reshape(passage_total, term_count)
    partial_value = lax.dot_general(
        masked, query_terms, (((1,), (1,)), ((), ())), preferred_element_type=jnp.float32
    )
    share = passage_total // groups
    parts = [
        lax.dynamic_slice_in_dim(partial_value, (y ^ k) * share, share, 0) for k in range(groups)
    ]
    scores = parts[0]
    for k in range(1, groups):
        scores = scores + lax.ppermute(parts[k], "y", [(i, i ^ k) for i in range(groups)])
    return doc_terms, scores.T


def solution(mesh):
    grid = Mesh(mesh.devices.reshape(4, 4, 8, CORES), ("y", "x", "z", "c"))
    docs = ("x", "z", "c")
    return jax.shard_map(
        local,
        mesh=grid,
        in_specs=(
            P(docs, "y", None),
            P(("y",) + docs, None),
            P(docs),
            P(docs, "y"),
            P(docs, "y", None),
        ),
        out_specs=(P(docs, "y"), P(docs, "y")),
        check_vma=False,
    )
```

```python
import functools

import jax
import jax.numpy as jnp
from jax import lax
from jax.experimental import pallas as pl
from jax.experimental.pallas import tpu as pltpu
from jax.sharding import Mesh, PartitionSpec as P

saturate = 1.2
length_slope = 0.75
CORES = 2
ALONG_X_FIRST = 32


def pool_kernel(block_count, piece_count, passages, rows, valid_ref, *refs):
    blocks = refs[:block_count]
    pieces = refs[block_count : block_count + piece_count]
    lens_ref, out_ref, held, weights, sums, block_sems, piece_sems = refs[block_count + piece_count :]
    per = passages * rows
    tile = sums.shape[2]
    starts = [sum(piece.shape[0] for piece in pieces[:k]) for k in range(piece_count)]
    owners = out_ref.shape[0] // passages
    each = block_count // owners
    piece_copies = [
        pltpu.make_async_copy(
            pieces[k],
            weights.at[pl.ds(starts[k], pieces[k].shape[0])],
            piece_sems.at[k],
        )
        for k in range(piece_count)
    ]
    block_copies = [
        pltpu.make_async_copy(
            blocks[b], held.at[b // each, pl.ds((b % each) * per, per)], block_sems.at[b]
        )
        for b in range(block_count)
    ]
    for copy in piece_copies + block_copies:
        copy.start()
    for copy in piece_copies + block_copies:
        copy.wait()
    row = lax.broadcasted_iota(jnp.int32, (8, tile), 0)
    tiles = weights.shape[0] // tile

    def one_part(part, _):
        owner, column = part // tiles, part % tiles
        logits = lax.dot_general(
            held[owner],
            weights[pl.ds(pl.multiple_of(column * tile, tile), tile), :],
            (((1,), (1,)), ((), ())),
            preferred_element_type=jnp.float32,
        )
        lines = []
        for p in range(passages):
            total = None
            for b in range(each):
                valid = valid_ref[(owner * each + b) * passages + p]
                grown = None
                for g in range(rows // 8):
                    at = b * per + p * rows + g * 8
                    x = jnp.where(row < valid - g * 8, jnp.maximum(logits[at : at + 8], 0.0), 0.0)
                    grown = x if grown is None else grown + (x + grown * x)
                shifted = 1.0 + grown
                small = shifted == 1.0
                ratio = grown / jnp.where(small, 1.0, shifted - 1.0)
                logs = jnp.where(small, grown, jnp.log(shifted) * ratio)
                total = logs if total is None else total + logs
            lines.append(jnp.sum(total, axis=0, keepdims=True))
        sums[part] = jnp.concatenate(lines, axis=0)
        return 0

    lax.fori_loop(0, owners * tiles, one_part, 0)
    for owner in range(owners):
        span = slice(owner * passages, (owner + 1) * passages)
        for column in range(tiles):
            out_ref[span, column * tile : (column + 1) * tile] = (
                sums[owner * tiles + column] / lens_ref[span, :1]
            ).astype(out_ref.dtype)


def pooled_terms(blocks, valid, lens_wide, pieces, rows, tile=256):
    count = len(blocks)
    width = blocks[0].shape[1]
    terms, lines = sum(p.shape[0] for p in pieces), lens_wide.shape[0]
    owners = CORES
    passages = lines // owners
    anywhere = pl.BlockSpec(memory_space=pltpu.HBM)
    return pl.pallas_call(
        functools.partial(pool_kernel, count, len(pieces), passages, rows),
        grid_spec=pltpu.PrefetchScalarGridSpec(
            num_scalar_prefetch=1,
            grid=(1,),
            in_specs=[anywhere] * (count + len(pieces))
            + [pl.BlockSpec((lines, 128), lambda i, v: (0, 0))],
            out_specs=pl.BlockSpec((lines, terms), lambda i, v: (0, 0)),
            scratch_shapes=[
                pltpu.VMEM((owners, count // owners * passages * rows, width), jnp.bfloat16),
                pltpu.VMEM((terms, width), jnp.bfloat16),
                pltpu.VMEM((owners * (terms // tile), passages, tile), jnp.float32),
                pltpu.SemaphoreType.DMA((count,)),
                pltpu.SemaphoreType.DMA((len(pieces),)),
            ],
        ),
        out_shape=jax.ShapeDtypeStruct((lines, terms), jnp.bfloat16),
        compiler_params=pltpu.CompilerParams(vmem_limit_bytes=40 << 20),
    )(valid, *blocks, *pieces, lens_wide)


def steps(size, toward):
    return [
        (i * CORES + c, ((i + (toward if c == 0 else -toward)) % size) * CORES + c)
        for i in range(size)
        for c in range(CORES)
    ]


def swap_cores(a):
    return lax.ppermute(a, "c", [(0, 1), (1, 0)])


def hop(a, axis, toward):
    return lax.ppermute(a, (axis, "c"), steps(lax.axis_size(axis), toward))


def ring4(a, axis):
    ahead, behind = hop(a, axis, 1), hop(a, axis, -1)
    return [a, ahead, behind, hop(ahead, axis, 1)]


SHIFTS4 = (0, -1, 1, -2)
SHIFTS8 = (0, -1, 1, -2, 2, -3, 3, -4)


def placed(pooled, tile, tiles):
    onehot = (tile[:, None] == jnp.arange(tiles)[None, :]).astype(jnp.bfloat16)
    return jnp.einsum(
        "prk,rt->ptk",
        pooled.reshape(pooled.shape[0], tile.shape[0], -1),
        onehot,
        preferred_element_type=jnp.float32,
    ).astype(jnp.bfloat16)


def after(value, *others):
    return lax.optimization_barrier((value,) + others)[0]


def local(hidden, w_vocab, lengths, query_terms, tile_routes):
    groups = lax.axis_size("y")
    members = lax.axis_size("x") * lax.axis_size("z") * CORES
    docs = ("x", "z", "c")
    local_count, rows, _ = hidden.shape
    y, core = lax.axis_index("y"), lax.axis_index("c")

    at_x, at_z = lax.axis_index("x"), lax.axis_index("z")
    sign = 1 - 2 * core
    first_x, first_z = w_vocab[:ALONG_X_FIRST], w_vocab[ALONG_X_FIRST:]
    p1, s1 = hop(first_z, "z", 1), hop(first_z, "z", -1)
    line = jnp.concatenate(ring4(first_x, "x"))
    by_line = lax.all_gather(after(line, p1, s1), "z", axis=0, tiled=True)
    own = ring4(hidden, "y")
    other = [swap_cores(a) for a in own]
    p2 = hop(p1, "z", 1)
    near = ring4(jnp.concatenate([first_z, p1, s1, p2]), "x")
    s2, p3 = hop(s1, "z", -1), hop(p2, "z", 1)
    s3, p4 = hop(s2, "z", -1), hop(after(p3, own[1], own[2]), "z", 1)
    far = ring4(after(jnp.concatenate([s2, p3, s3, p4]), near[1], near[2]), "x")

    lens_pair = jnp.stack([lengths, swap_cores(lengths)])
    shifts = sign * jnp.array(SHIFTS4, jnp.int32)
    places = jnp.stack([(y + shifts) % groups, (y - shifts) % groups])
    valid = jnp.clip(lens_pair[:, None, :] - places[:, :, None] * rows, 0, rows).reshape(-1)
    blocks_in = [a.reshape(local_count * rows, -1) for a in own + other]

    lens_flat = lens_pair.reshape(-1).astype(jnp.float32)
    lens_wide = jnp.broadcast_to(lens_flat[:, None], (lens_flat.shape[0], 128))
    depth = lax.axis_size("z")
    tiles_x = (at_x + shifts) % lax.axis_size("x") * depth
    around = sign * jnp.array(SHIFTS8, jnp.int32)
    tiles_z = (at_z + around) % depth
    half = len(SHIFTS8) // 2
    line_tiles = (jnp.arange(depth)[:, None] + tiles_x[None, :]).reshape(-1)
    near_tiles = (tiles_x[:, None] + tiles_z[None, :half]).reshape(-1)
    far_tiles = (tiles_x[:, None] + tiles_z[None, half:]).reshape(-1)
    term_count = query_terms.shape[1]
    tile_count = term_count // 128
    from_near = pooled_terms(blocks_in, valid, lens_wide, near, rows)
    from_line = pooled_terms(blocks_in, valid, lens_wide, [by_line], rows)
    from_far = pooled_terms(blocks_in, valid, lens_wide, far, rows)
    from_line = placed(from_line, line_tiles, tile_count)
    from_both = placed(
        jnp.concatenate([from_near, from_far], axis=1),
        jnp.concatenate([near_tiles, far_tiles]),
        tile_count,
    )
    pooled = jnp.concatenate([from_line, from_both], axis=2)
    mine = pooled[:local_count, :, None]
    theirs = swap_cores(pooled[local_count:])[:, :, None]
    blocks = jnp.where(
        core == 0,
        jnp.concatenate([mine, theirs], axis=2),
        jnp.concatenate([theirs, mine], axis=2),
    ).reshape(local_count, tile_count, 128)
    doc_terms = blocks.reshape(local_count, term_count)

    my_routes = tile_routes[0]
    capacity = min(tile_count, 4)
    passage_total = members * local_count
    owners = lax.broadcasted_iota(jnp.int32, (1, 1, members), 2)
    is_listed = jnp.any(my_routes[:, :, None] == owners, axis=1)
    earlier = lax.broadcasted_iota(jnp.int32, (tile_count, tile_count), 0)
    later = lax.broadcasted_iota(jnp.int32, (tile_count, tile_count), 1)
    slot_index = (
        lax.dot_general(
            (earlier <= later).astype(jnp.bfloat16),
            is_listed.astype(jnp.bfloat16),
            (((0,), (0,)), ((), ())),
            preferred_element_type=jnp.float32,
        ).astype(jnp.int32)
        - 1
    )
    slot_ids = lax.broadcasted_iota(jnp.int32, (1, capacity, 1), 1)
    selector = (is_listed.T[:, None, :] & (slot_index.T[:, None, :] == slot_ids)).astype(
        jnp.bfloat16
    )
    lane = lax.broadcasted_iota(jnp.int32, (1, 1, 128), 2)
    numbers = jnp.where(
        lane == 0, lax.broadcasted_iota(jnp.int32, (1, tile_count, 128), 1), 0
    ).astype(jnp.bfloat16)
    outgoing = jnp.einsum(
        "oct,ptk->ocpk",
        selector,
        jnp.concatenate([blocks, numbers], axis=0),
        preferred_element_type=jnp.float32,
    )
    line_at = lax.broadcasted_iota(jnp.int32, (local_count + 1, 128), 0)
    lane_at = lax.broadcasted_iota(jnp.int32, (local_count + 1, 128), 1)
    lens_line = jnp.zeros((local_count + 1, 128), jnp.float32)
    for p in range(local_count):
        lens_line = jnp.where(
            (line_at == local_count) & (lane_at == p + 1), lengths[p].astype(jnp.float32), lens_line
        )
    outgoing = (outgoing + lens_line).astype(jnp.bfloat16)
    arrived = lax.all_to_all(outgoing, docs, split_axis=0, concat_axis=0, tiled=True)
    notes = arrived[:, :, local_count, :].astype(jnp.float32)
    lens_in = notes[:, 0, 1 : local_count + 1]
    average = jnp.sum(lens_in) / passage_total
    denominator = saturate * (1.0 - length_slope + length_slope * lens_in / average)
    weight = arrived[:, :, :local_count, :].astype(jnp.float32)
    scaled = (
        weight * (saturate + 1.0) / (weight + denominator[:, None, :, None])
    ).astype(jnp.bfloat16)
    tile_ids = lax.broadcasted_iota(jnp.float32, (1, 1, tile_count), 2)
    placing = (notes[:, :, :1] == tile_ids).astype(jnp.bfloat16)
    masked = jnp.einsum(
        "bct,bcpk->bptk", placing, scaled, preferred_element_type=jnp.float32
    ).astype(jnp.bfloat16)
    masked = masked.reshape(passage_total, term_count)
    partial_value = lax.dot_general(
        masked, query_terms, (((1,), (1,)), ((), ())), preferred_element_type=jnp.float32
    )
    share = passage_total // groups
    parts = [
        lax.dynamic_slice_in_dim(partial_value, (y ^ k) * share, share, 0) for k in range(groups)
    ]
    scores = parts[0]
    for k in range(1, groups):
        scores = scores + lax.ppermute(parts[k], "y", [(i, i ^ k) for i in range(groups)])
    return doc_terms, scores.T


def solution(mesh):
    grid = Mesh(mesh.devices.reshape(4, 4, 8, CORES), ("y", "x", "z", "c"))
    docs = ("x", "z", "c")
    return jax.shard_map(
        local,
        mesh=grid,
        in_specs=(
            P(docs, "y", None),
            P(("y",) + docs, None),
            P(docs),
            P(docs, "y"),
            P(docs, "y", None),
        ),
        out_specs=(P(docs, "y"), P(docs, "y")),
        check_vma=False,
    )
```

```python
import functools

import jax
import jax.numpy as jnp
from jax import lax
from jax.experimental import pallas as pl
from jax.experimental.pallas import tpu as pltpu
from jax.sharding import Mesh, PartitionSpec as P

saturate = 1.2
length_slope = 0.75
CORES = 2
ALONG_X_FIRST = 32


def pool_kernel(block_count, piece_count, passages, rows, valid_ref, *refs):
    blocks = refs[:block_count]
    pieces = refs[block_count : block_count + piece_count]
    lens_ref, out_ref, held, weights, sums, block_sems, piece_sems = refs[block_count + piece_count :]
    per = passages * rows
    tile = sums.shape[2]
    owners = out_ref.shape[0] // passages
    each = block_count // owners
    tiles = weights.shape[0] // tile
    block_copies = [
        pltpu.make_async_copy(
            blocks[b], held.at[b // each, pl.ds((b % each) * per, per)], block_sems.at[b]
        )
        for b in range(block_count)
    ]
    tile_copies = [[] for _ in range(tiles)]
    at, number = 0, 0
    for k in range(piece_count):
        size = pieces[k].shape[0]
        done = 0
        while done < size:
            span = min(size - done, tile - at % tile)
            tile_copies[at // tile].append(
                pltpu.make_async_copy(
                    pieces[k].at[pl.ds(done, span)],
                    weights.at[pl.ds(at, span)],
                    piece_sems.at[number],
                )
            )
            at, done, number = at + span, done + span, number + 1
    for copy in block_copies[:each] + tile_copies[0] + tile_copies[1]:
        copy.start()
    row = lax.broadcasted_iota(jnp.int32, (8, tile), 0)

    def one_part(part, _):
        owner, column = part // tiles, part % tiles
        for k in range(tiles):

            @pl.when(part == k)
            def _():
                if k == 0:
                    for copy in block_copies[:each]:
                        copy.wait()
                for copy in tile_copies[k]:
                    copy.wait()
                if k + 2 < tiles:
                    for copy in tile_copies[k + 2]:
                        copy.start()
                later = block_copies[each:]
                share = -(-len(later) // (tiles - 1))
                for copy in later[k * share : (k + 1) * share]:
                    copy.start()

        @pl.when(part == tiles)
        def _():
            for copy in block_copies[each:]:
                copy.wait()

        logits = lax.dot_general(
            held[owner],
            weights[pl.ds(pl.multiple_of(column * tile, tile), tile), :],
            (((1,), (1,)), ((), ())),
            preferred_element_type=jnp.float32,
        )
        lines = []
        for p in range(passages):
            total = None
            for b in range(each):
                valid = valid_ref[(owner * each + b) * passages + p]
                grown = None
                for g in range(rows // 8):
                    at = b * per + p * rows + g * 8
                    x = jnp.where(row < valid - g * 8, jnp.maximum(logits[at : at + 8], 0.0), 0.0)
                    grown = x if grown is None else grown + (x + grown * x)
                shifted = 1.0 + grown
                small = shifted == 1.0
                ratio = grown / jnp.where(small, 1.0, shifted - 1.0)
                logs = jnp.where(small, grown, jnp.log(shifted) * ratio)
                total = logs if total is None else total + logs
            lines.append(jnp.sum(total, axis=0, keepdims=True))
        sums[part] = jnp.concatenate(lines, axis=0)
        return 0

    lax.fori_loop(0, owners * tiles, one_part, 0)
    for owner in range(owners):
        span = slice(owner * passages, (owner + 1) * passages)
        for column in range(tiles):
            out_ref[span, column * tile : (column + 1) * tile] = (
                sums[owner * tiles + column] / lens_ref[span, :1]
            ).astype(out_ref.dtype)


def pooled_terms(blocks, valid, lens_wide, pieces, rows, tile=256):
    count = len(blocks)
    width = blocks[0].shape[1]
    terms, lines = sum(p.shape[0] for p in pieces), lens_wide.shape[0]
    owners = CORES
    passages = lines // owners
    anywhere = pl.BlockSpec(memory_space=pltpu.HBM)
    return pl.pallas_call(
        functools.partial(pool_kernel, count, len(pieces), passages, rows),
        grid_spec=pltpu.PrefetchScalarGridSpec(
            num_scalar_prefetch=1,
            grid=(1,),
            in_specs=[anywhere] * (count + len(pieces))
            + [pl.BlockSpec((lines, 128), lambda i, v: (0, 0))],
            out_specs=pl.BlockSpec((lines, terms), lambda i, v: (0, 0)),
            scratch_shapes=[
                pltpu.VMEM((owners, count // owners * passages * rows, width), jnp.bfloat16),
                pltpu.VMEM((terms, width), jnp.bfloat16),
                pltpu.VMEM((owners * (terms // tile), passages, tile), jnp.float32),
                pltpu.SemaphoreType.DMA((count,)),
                pltpu.SemaphoreType.DMA((len(pieces) + terms // tile,)),
            ],
        ),
        out_shape=jax.ShapeDtypeStruct((lines, terms), jnp.bfloat16),
        cost_estimate=pl.CostEstimate(
            flops=2 * count * passages * rows * width * terms,
            bytes_accessed=2 * width * (count * passages * rows + terms),
            transcendentals=count * passages * terms * 8,
        ),
        compiler_params=pltpu.CompilerParams(vmem_limit_bytes=40 << 20),
    )(valid, *blocks, *pieces, lens_wide)


def steps(size, toward):
    return [
        (i * CORES + c, ((i + (toward if c == 0 else -toward)) % size) * CORES + c)
        for i in range(size)
        for c in range(CORES)
    ]


def swap_cores(a):
    return lax.ppermute(a, "c", [(0, 1), (1, 0)])


def hop(a, axis, toward):
    return lax.ppermute(a, (axis, "c"), steps(lax.axis_size(axis), toward))


def ring4(a, axis):
    ahead, behind = hop(a, axis, 1), hop(a, axis, -1)
    return [a, ahead, behind, hop(ahead, axis, 1)]


SHIFTS4 = (0, -1, 1, -2)
SHIFTS8 = (0, -1, 1, -2, 2, -3, 3, -4)


def placed(pooled, tile, tiles):
    onehot = (tile[:, None] == jnp.arange(tiles)[None, :]).astype(jnp.bfloat16)
    return jnp.einsum(
        "prk,rt->ptk",
        pooled.reshape(pooled.shape[0], tile.shape[0], -1),
        onehot,
        preferred_element_type=jnp.float32,
    ).astype(jnp.bfloat16)


def after(value, *others):
    return lax.optimization_barrier((value,) + others)[0]


def local(hidden, w_vocab, lengths, query_terms, tile_routes):
    groups = lax.axis_size("y")
    members = lax.axis_size("x") * lax.axis_size("z") * CORES
    docs = ("x", "z", "c")
    local_count, rows, _ = hidden.shape
    y, core = lax.axis_index("y"), lax.axis_index("c")

    at_x, at_z = lax.axis_index("x"), lax.axis_index("z")
    sign = 1 - 2 * core
    first_x, first_z = w_vocab[:ALONG_X_FIRST], w_vocab[ALONG_X_FIRST:]
    p1, s1 = hop(first_z, "z", 1), hop(first_z, "z", -1)
    line = jnp.concatenate(ring4(first_x, "x"))
    by_line = lax.all_gather(after(line, p1, s1), "z", axis=0, tiled=True)
    own = ring4(hidden, "y")
    other = [swap_cores(a) for a in own]
    p2 = hop(p1, "z", 1)
    near = ring4(jnp.concatenate([first_z, p1, s1, p2]), "x")
    s2, p3 = hop(s1, "z", -1), hop(p2, "z", 1)
    s3, p4 = hop(s2, "z", -1), hop(after(p3, own[1], own[2]), "z", 1)
    far = ring4(after(jnp.concatenate([s2, p3, s3, p4]), near[1], near[2]), "x")

    lens_pair = jnp.stack([lengths, swap_cores(lengths)])
    shifts = sign * jnp.array(SHIFTS4, jnp.int32)
    places = jnp.stack([(y + shifts) % groups, (y - shifts) % groups])
    valid = jnp.clip(lens_pair[:, None, :] - places[:, :, None] * rows, 0, rows).reshape(-1)
    blocks_in = [a.reshape(local_count * rows, -1) for a in own + other]

    lens_flat = lens_pair.reshape(-1).astype(jnp.float32)
    lens_wide = jnp.broadcast_to(lens_flat[:, None], (lens_flat.shape[0], 128))
    depth = lax.axis_size("z")
    tiles_x = (at_x + shifts) % lax.axis_size("x") * depth
    around = sign * jnp.array(SHIFTS8, jnp.int32)
    tiles_z = (at_z + around) % depth
    half = len(SHIFTS8) // 2
    line_tiles = (jnp.arange(depth)[:, None] + tiles_x[None, :]).reshape(-1)
    near_tiles = (tiles_x[:, None] + tiles_z[None, :half]).reshape(-1)
    far_tiles = (tiles_x[:, None] + tiles_z[None, half:]).reshape(-1)
    term_count = query_terms.shape[1]
    tile_count = term_count // 128
    most = pooled_terms(blocks_in, valid, lens_wide, near + [by_line], rows)
    from_near, from_line = jnp.split(most, [4 * near[0].shape[0]], axis=1)
    from_far = pooled_terms(blocks_in, valid, lens_wide, far, rows)
    from_line = placed(from_line, line_tiles, tile_count)
    from_both = placed(
        jnp.concatenate([from_near, from_far], axis=1),
        jnp.concatenate([near_tiles, far_tiles]),
        tile_count,
    )
    pooled = jnp.concatenate([from_line, from_both], axis=2)
    mine = pooled[:local_count, :, None]
    theirs = swap_cores(pooled[local_count:])[:, :, None]
    blocks = jnp.where(
        core == 0,
        jnp.concatenate([mine, theirs], axis=2),
        jnp.concatenate([theirs, mine], axis=2),
    ).reshape(local_count, tile_count, 128)
    doc_terms = blocks.reshape(local_count, term_count)

    my_routes = tile_routes[0]
    capacity = min(tile_count, 4)
    passage_total = members * local_count
    owners = lax.broadcasted_iota(jnp.int32, (1, 1, members), 2)
    is_listed = jnp.any(my_routes[:, :, None] == owners, axis=1)
    earlier = lax.broadcasted_iota(jnp.int32, (tile_count, tile_count), 0)
    later = lax.broadcasted_iota(jnp.int32, (tile_count, tile_count), 1)
    slot_index = (
        lax.dot_general(
            (earlier <= later).astype(jnp.bfloat16),
            is_listed.astype(jnp.bfloat16),
            (((0,), (0,)), ((), ())),
            preferred_element_type=jnp.float32,
        ).astype(jnp.int32)
        - 1
    )
    slot_ids = lax.broadcasted_iota(jnp.int32, (1, capacity, 1), 1)
    selector = (is_listed.T[:, None, :] & (slot_index.T[:, None, :] == slot_ids)).astype(
        jnp.bfloat16
    )
    lane = lax.broadcasted_iota(jnp.int32, (1, 1, 128), 2)
    numbers = jnp.where(
        lane == 0, lax.broadcasted_iota(jnp.int32, (1, tile_count, 128), 1), 0
    ).astype(jnp.bfloat16)
    outgoing = jnp.einsum(
        "oct,ptk->ocpk",
        selector,
        jnp.concatenate([blocks, numbers], axis=0),
        preferred_element_type=jnp.float32,
    )
    line_at = lax.broadcasted_iota(jnp.int32, (local_count + 1, 128), 0)
    lane_at = lax.broadcasted_iota(jnp.int32, (local_count + 1, 128), 1)
    lens_line = jnp.zeros((local_count + 1, 128), jnp.float32)
    for p in range(local_count):
        lens_line = jnp.where(
            (line_at == local_count) & (lane_at == p + 1), lengths[p].astype(jnp.float32), lens_line
        )
    outgoing = (outgoing + lens_line).astype(jnp.bfloat16)
    arrived = lax.all_to_all(outgoing, docs, split_axis=0, concat_axis=0, tiled=True)
    notes = arrived[:, :, local_count, :].astype(jnp.float32)
    lens_in = notes[:, 0, 1 : local_count + 1]
    average = jnp.sum(lens_in) / passage_total
    denominator = saturate * (1.0 - length_slope + length_slope * lens_in / average)
    weight = arrived[:, :, :local_count, :].astype(jnp.float32)
    scaled = (
        weight * (saturate + 1.0) / (weight + denominator[:, None, :, None])
    ).astype(jnp.bfloat16)
    tile_ids = lax.broadcasted_iota(jnp.float32, (1, 1, tile_count), 2)
    placing = (notes[:, :, :1] == tile_ids).astype(jnp.bfloat16)
    masked = jnp.einsum(
        "bct,bcpk->bptk", placing, scaled, preferred_element_type=jnp.float32
    ).astype(jnp.bfloat16)
    masked = masked.reshape(passage_total, term_count)
    partial_value = lax.dot_general(
        masked, query_terms, (((1,), (1,)), ((), ())), preferred_element_type=jnp.float32
    )
    share = passage_total // groups
    parts = [
        lax.dynamic_slice_in_dim(partial_value, (y ^ k) * share, share, 0) for k in range(groups)
    ]
    scores = parts[0]
    for k in range(1, groups):
        scores = scores + lax.ppermute(parts[k], "y", [(i, i ^ k) for i in range(groups)])
    return doc_terms, scores.T


def solution(mesh):
    grid = Mesh(mesh.devices.reshape(4, 4, 8, CORES), ("y", "x", "z", "c"))
    docs = ("x", "z", "c")
    return jax.shard_map(
        local,
        mesh=grid,
        in_specs=(
            P(docs, "y", None),
            P(("y",) + docs, None),
            P(docs),
            P(docs, "y"),
            P(docs, "y", None),
        ),
        out_specs=(P(docs, "y"), P(docs, "y")),
        check_vma=False,
    )
```

```python
import functools

import jax
import jax.numpy as jnp
from jax import lax
from jax.experimental import pallas as pl
from jax.experimental.pallas import tpu as pltpu
from jax.sharding import Mesh, PartitionSpec as P

saturate = 1.2
length_slope = 0.75
CORES = 2
ALONG_X_FIRST = 32


def pool_kernel(block_count, piece_count, passages, rows, valid_ref, *refs):
    blocks = refs[:block_count]
    pieces = refs[block_count : block_count + piece_count]
    lens_ref, out_ref, held, weights, sums, block_sems, piece_sems = refs[block_count + piece_count :]
    per = passages * rows
    tile = sums.shape[2]
    owners = out_ref.shape[0] // passages
    each = block_count // owners
    tiles = weights.shape[0] // tile
    block_copies = [
        pltpu.make_async_copy(
            blocks[b], held.at[b // each, pl.ds((b % each) * per, per)], block_sems.at[b]
        )
        for b in range(block_count)
    ]
    tile_copies = [[] for _ in range(tiles)]
    at, number = 0, 0
    for k in range(piece_count):
        size = pieces[k].shape[0]
        done = 0
        while done < size:
            span = min(size - done, tile - at % tile)
            tile_copies[at // tile].append(
                pltpu.make_async_copy(
                    pieces[k].at[pl.ds(done, span)],
                    weights.at[pl.ds(at, span)],
                    piece_sems.at[number],
                )
            )
            at, done, number = at + span, done + span, number + 1
    for copy in block_copies[:each] + tile_copies[0] + tile_copies[1]:
        copy.start()
    row = lax.broadcasted_iota(jnp.int32, (8, tile), 0)

    def one_part(part, _):
        owner, column = part // tiles, part % tiles
        for k in range(tiles):

            @pl.when(part == k)
            def _():
                if k == 0:
                    for copy in block_copies[:each]:
                        copy.wait()
                for copy in tile_copies[k]:
                    copy.wait()
                if k + 2 < tiles:
                    for copy in tile_copies[k + 2]:
                        copy.start()
                later = block_copies[each:]
                share = -(-len(later) // (tiles - 1))
                for copy in later[k * share : (k + 1) * share]:
                    copy.start()

        @pl.when(part == tiles)
        def _():
            for copy in block_copies[each:]:
                copy.wait()

        logits = lax.dot_general(
            held[owner],
            weights[pl.ds(pl.multiple_of(column * tile, tile), tile), :],
            (((1,), (1,)), ((), ())),
            preferred_element_type=jnp.float32,
        )
        lines = []
        for p in range(passages):
            total = None
            for b in range(each):
                valid = valid_ref[(owner * each + b) * passages + p]
                grown = None
                for g in range(rows // 8):
                    at = b * per + p * rows + g * 8
                    x = jnp.where(row < valid - g * 8, jnp.maximum(logits[at : at + 8], 0.0), 0.0)
                    grown = x if grown is None else grown + (x + grown * x)
                shifted = 1.0 + grown
                small = shifted == 1.0
                ratio = grown / jnp.where(small, 1.0, shifted - 1.0)
                logs = jnp.where(small, grown, jnp.log(shifted) * ratio)
                total = logs if total is None else total + logs
            lines.append(jnp.sum(total, axis=0, keepdims=True))
        sums[part] = jnp.concatenate(lines, axis=0)
        return 0

    lax.fori_loop(0, owners * tiles, one_part, 0)
    for owner in range(owners):
        span = slice(owner * passages, (owner + 1) * passages)
        for column in range(tiles):
            out_ref[span, column * tile : (column + 1) * tile] = (
                sums[owner * tiles + column] / lens_ref[span, :1]
            ).astype(out_ref.dtype)


def pooled_terms(blocks, valid, lens_wide, pieces, rows, tile=256):
    count = len(blocks)
    width = blocks[0].shape[1]
    terms, lines = sum(p.shape[0] for p in pieces), lens_wide.shape[0]
    owners = CORES
    passages = lines // owners
    anywhere = pl.BlockSpec(memory_space=pltpu.HBM)
    return pl.pallas_call(
        functools.partial(pool_kernel, count, len(pieces), passages, rows),
        grid_spec=pltpu.PrefetchScalarGridSpec(
            num_scalar_prefetch=1,
            grid=(1,),
            in_specs=[anywhere] * (count + len(pieces))
            + [pl.BlockSpec((lines, 128), lambda i, v: (0, 0))],
            out_specs=pl.BlockSpec((lines, terms), lambda i, v: (0, 0)),
            scratch_shapes=[
                pltpu.VMEM((owners, count // owners * passages * rows, width), jnp.bfloat16),
                pltpu.VMEM((terms, width), jnp.bfloat16),
                pltpu.VMEM((owners * (terms // tile), passages, tile), jnp.float32),
                pltpu.SemaphoreType.DMA((count,)),
                pltpu.SemaphoreType.DMA((len(pieces) + terms // tile,)),
            ],
        ),
        out_shape=jax.ShapeDtypeStruct((lines, terms), jnp.bfloat16),
        cost_estimate=pl.CostEstimate(
            flops=2 * count * passages * rows * width * terms,
            bytes_accessed=2 * width * (count * passages * rows + terms),
            transcendentals=count * passages * terms * 8,
        ),
        compiler_params=pltpu.CompilerParams(vmem_limit_bytes=40 << 20),
    )(valid, *blocks, *pieces, lens_wide)


def steps(size, toward):
    return [
        (i * CORES + c, ((i + (toward if c == 0 else -toward)) % size) * CORES + c)
        for i in range(size)
        for c in range(CORES)
    ]


def swap_cores(a):
    return lax.ppermute(a, "c", [(0, 1), (1, 0)])


def hop(a, axis, toward):
    return lax.ppermute(a, (axis, "c"), steps(lax.axis_size(axis), toward))


def ring4(a, axis):
    ahead, behind = hop(a, axis, 1), hop(a, axis, -1)
    return [a, ahead, behind, hop(ahead, axis, 1)]


SHIFTS4 = (0, -1, 1, -2)
SHIFTS8 = (0, -1, 1, -2, 2, -3, 3, -4)


def placed(pooled, tile, tiles):
    onehot = (tile[:, None] == jnp.arange(tiles)[None, :]).astype(jnp.bfloat16)
    return jnp.einsum(
        "prk,rt->ptk",
        pooled.reshape(pooled.shape[0], tile.shape[0], -1),
        onehot,
        preferred_element_type=jnp.float32,
    ).astype(jnp.bfloat16)


def after(value, *others):
    return lax.optimization_barrier((value,) + others)[0]


def local(hidden, w_vocab, lengths, query_terms, tile_routes):
    groups = lax.axis_size("y")
    members = lax.axis_size("x") * lax.axis_size("z") * CORES
    docs = ("x", "z", "c")
    local_count, rows, _ = hidden.shape
    y, core = lax.axis_index("y"), lax.axis_index("c")

    at_x, at_z = lax.axis_index("x"), lax.axis_index("z")
    sign = 1 - 2 * core
    first_x, first_z = w_vocab[:ALONG_X_FIRST], w_vocab[ALONG_X_FIRST:]
    p1, s1 = hop(first_z, "z", 1), hop(first_z, "z", -1)
    line = jnp.concatenate(ring4(first_x, "x"))
    by_line = lax.all_gather(after(line, p1, s1), "z", axis=0, tiled=True)
    by_line = pltpu.with_memory_space_constraint(by_line, pltpu.HBM)
    own = ring4(hidden, "y")
    other = [swap_cores(a) for a in own]
    p2 = hop(p1, "z", 1)
    near = ring4(jnp.concatenate([first_z, p1, s1, p2]), "x")
    s2, p3 = hop(s1, "z", -1), hop(p2, "z", 1)
    s3, p4 = hop(s2, "z", -1), hop(after(p3, own[1], own[2]), "z", 1)
    far = ring4(after(jnp.concatenate([s2, p3, s3, p4]), near[1], near[2]), "x")

    lens_pair = jnp.stack([lengths, swap_cores(lengths)])
    shifts = sign * jnp.array(SHIFTS4, jnp.int32)
    places = jnp.stack([(y + shifts) % groups, (y - shifts) % groups])
    valid = jnp.clip(lens_pair[:, None, :] - places[:, :, None] * rows, 0, rows).reshape(-1)
    blocks_in = [a.reshape(local_count * rows, -1) for a in own + other]

    lens_flat = lens_pair.reshape(-1).astype(jnp.float32)
    lens_wide = jnp.broadcast_to(lens_flat[:, None], (lens_flat.shape[0], 128))
    depth = lax.axis_size("z")
    tiles_x = (at_x + shifts) % lax.axis_size("x") * depth
    around = sign * jnp.array(SHIFTS8, jnp.int32)
    tiles_z = (at_z + around) % depth
    half = len(SHIFTS8) // 2
    line_tiles = (jnp.arange(depth)[:, None] + tiles_x[None, :]).reshape(-1)
    near_tiles = (tiles_x[:, None] + tiles_z[None, :half]).reshape(-1)
    far_tiles = (tiles_x[:, None] + tiles_z[None, half:]).reshape(-1)
    term_count = query_terms.shape[1]
    tile_count = term_count // 128
    most = pooled_terms(blocks_in, valid, lens_wide, near + [by_line], rows)
    from_near, from_line = jnp.split(most, [4 * near[0].shape[0]], axis=1)
    from_far = pooled_terms(blocks_in, valid, lens_wide, far, rows)
    from_line = placed(from_line, line_tiles, tile_count)
    from_both = placed(
        jnp.concatenate([from_near, from_far], axis=1),
        jnp.concatenate([near_tiles, far_tiles]),
        tile_count,
    )
    pooled = jnp.concatenate([from_line, from_both], axis=2)
    mine = pooled[:local_count, :, None]
    theirs = swap_cores(pooled[local_count:])[:, :, None]
    blocks = jnp.where(
        core == 0,
        jnp.concatenate([mine, theirs], axis=2),
        jnp.concatenate([theirs, mine], axis=2),
    ).reshape(local_count, tile_count, 128)
    doc_terms = blocks.reshape(local_count, term_count)

    my_routes = tile_routes[0]
    capacity = min(tile_count, 4)
    passage_total = members * local_count
    owners = lax.broadcasted_iota(jnp.int32, (1, 1, members), 2)
    is_listed = jnp.any(my_routes[:, :, None] == owners, axis=1)
    earlier = lax.broadcasted_iota(jnp.int32, (tile_count, tile_count), 0)
    later = lax.broadcasted_iota(jnp.int32, (tile_count, tile_count), 1)
    slot_index = (
        lax.dot_general(
            (earlier <= later).astype(jnp.bfloat16),
            is_listed.astype(jnp.bfloat16),
            (((0,), (0,)), ((), ())),
            preferred_element_type=jnp.float32,
        ).astype(jnp.int32)
        - 1
    )
    slot_ids = lax.broadcasted_iota(jnp.int32, (1, capacity, 1), 1)
    selector = (is_listed.T[:, None, :] & (slot_index.T[:, None, :] == slot_ids)).astype(
        jnp.bfloat16
    )
    lane = lax.broadcasted_iota(jnp.int32, (1, 1, 128), 2)
    numbers = jnp.where(
        lane == 0, lax.broadcasted_iota(jnp.int32, (1, tile_count, 128), 1), 0
    ).astype(jnp.bfloat16)
    outgoing = jnp.einsum(
        "oct,ptk->ocpk",
        selector,
        jnp.concatenate([blocks, numbers], axis=0),
        preferred_element_type=jnp.float32,
    )
    line_at = lax.broadcasted_iota(jnp.int32, (local_count + 1, 128), 0)
    lane_at = lax.broadcasted_iota(jnp.int32, (local_count + 1, 128), 1)
    lens_line = jnp.zeros((local_count + 1, 128), jnp.float32)
    for p in range(local_count):
        lens_line = jnp.where(
            (line_at == local_count) & (lane_at == p + 1), lengths[p].astype(jnp.float32), lens_line
        )
    outgoing = (outgoing + lens_line).astype(jnp.bfloat16)
    arrived = lax.all_to_all(outgoing, docs, split_axis=0, concat_axis=0, tiled=True)
    notes = arrived[:, :, local_count, :].astype(jnp.float32)
    lens_in = notes[:, 0, 1 : local_count + 1]
    average = jnp.sum(lens_in) / passage_total
    denominator = saturate * (1.0 - length_slope + length_slope * lens_in / average)
    weight = arrived[:, :, :local_count, :].astype(jnp.float32)
    scaled = (
        weight * (saturate + 1.0) / (weight + denominator[:, None, :, None])
    ).astype(jnp.bfloat16)
    tile_ids = lax.broadcasted_iota(jnp.float32, (1, 1, tile_count), 2)
    placing = (notes[:, :, :1] == tile_ids).astype(jnp.bfloat16)
    masked = jnp.einsum(
        "bct,bcpk->bptk", placing, scaled, preferred_element_type=jnp.float32
    ).astype(jnp.bfloat16)
    masked = masked.reshape(passage_total, term_count)
    partial_value = lax.dot_general(
        masked, query_terms, (((1,), (1,)), ((), ())), preferred_element_type=jnp.float32
    )
    share = passage_total // groups
    parts = [
        lax.dynamic_slice_in_dim(partial_value, (y ^ k) * share, share, 0) for k in range(groups)
    ]
    scores = parts[0]
    for k in range(1, groups):
        scores = scores + lax.ppermute(parts[k], "y", [(i, i ^ k) for i in range(groups)])
    return doc_terms, scores.T


def solution(mesh):
    grid = Mesh(mesh.devices.reshape(4, 4, 8, CORES), ("y", "x", "z", "c"))
    docs = ("x", "z", "c")
    return jax.shard_map(
        local,
        mesh=grid,
        in_specs=(
            P(docs, "y", None),
            P(("y",) + docs, None),
            P(docs),
            P(docs, "y"),
            P(docs, "y", None),
        ),
        out_specs=(P(docs, "y"), P(docs, "y")),
        check_vma=False,
    )
```

```python
import functools

import jax
import jax.numpy as jnp
from jax import lax
from jax.experimental import pallas as pl
from jax.experimental.pallas import tpu as pltpu
from jax.sharding import Mesh, PartitionSpec as P

saturate = 1.2
length_slope = 0.75
CORES = 2
ALONG_X_FIRST = 32


def pool_kernel(block_count, piece_count, passages, rows, valid_ref, *refs):
    blocks = refs[:block_count]
    pieces = refs[block_count : block_count + piece_count]
    lens_ref, out_ref, held, weights, sums, block_sems, piece_sems = refs[block_count + piece_count :]
    per = passages * rows
    tile = sums.shape[2]
    owners = out_ref.shape[0] // passages
    each = block_count // owners
    tiles = weights.shape[0] // tile
    block_copies = [
        pltpu.make_async_copy(
            blocks[b], held.at[b // each, pl.ds((b % each) * per, per)], block_sems.at[b]
        )
        for b in range(block_count)
    ]
    tile_copies = [[] for _ in range(tiles)]
    at, number = 0, 0
    for k in range(piece_count):
        size = pieces[k].shape[0]
        done = 0
        while done < size:
            span = min(size - done, tile - at % tile)
            tile_copies[at // tile].append(
                pltpu.make_async_copy(
                    pieces[k].at[pl.ds(done, span)],
                    weights.at[pl.ds(at, span)],
                    piece_sems.at[number],
                )
            )
            at, done, number = at + span, done + span, number + 1
    for copy in block_copies[:each] + tile_copies[0] + tile_copies[1]:
        copy.start()
    row = lax.broadcasted_iota(jnp.int32, (8, tile), 0)

    def one_part(part, _):
        owner, column = part // tiles, part % tiles
        for k in range(tiles):

            @pl.when(part == k)
            def _():
                if k == 0:
                    for copy in block_copies[:each]:
                        copy.wait()
                for copy in tile_copies[k]:
                    copy.wait()
                if k + 2 < tiles:
                    for copy in tile_copies[k + 2]:
                        copy.start()
                later = block_copies[each:]
                share = -(-len(later) // (tiles - 1))
                for copy in later[k * share : (k + 1) * share]:
                    copy.start()

        @pl.when(part == tiles)
        def _():
            for copy in block_copies[each:]:
                copy.wait()

        logits = lax.dot_general(
            held[owner],
            weights[pl.ds(pl.multiple_of(column * tile, tile), tile), :],
            (((1,), (1,)), ((), ())),
            preferred_element_type=jnp.float32,
        )
        lines = []
        for p in range(passages):
            total = None
            for b in range(each):
                valid = valid_ref[(owner * each + b) * passages + p]
                grown = None
                for g in range(rows // 8):
                    at = b * per + p * rows + g * 8
                    x = jnp.where(row < valid - g * 8, jnp.maximum(logits[at : at + 8], 0.0), 0.0)
                    grown = x if grown is None else grown + (x + grown * x)
                shifted = 1.0 + grown
                small = shifted == 1.0
                ratio = grown / jnp.where(small, 1.0, shifted - 1.0)
                logs = jnp.where(small, grown, jnp.log(shifted) * ratio)
                total = logs if total is None else total + logs
            lines.append(jnp.sum(total, axis=0, keepdims=True))
        sums[part] = jnp.concatenate(lines, axis=0)
        return 0

    lax.fori_loop(0, owners * tiles, one_part, 0)
    for owner in range(owners):
        span = slice(owner * passages, (owner + 1) * passages)
        for column in range(tiles):
            out_ref[span, column * tile : (column + 1) * tile] = (
                sums[owner * tiles + column] / lens_ref[span, :1]
            ).astype(out_ref.dtype)


def pooled_terms(blocks, valid, lens_wide, pieces, rows, tile=256):
    count = len(blocks)
    width = blocks[0].shape[1]
    terms, lines = sum(p.shape[0] for p in pieces), lens_wide.shape[0]
    owners = CORES
    passages = lines // owners
    anywhere = pl.BlockSpec(memory_space=pltpu.HBM)
    return pl.pallas_call(
        functools.partial(pool_kernel, count, len(pieces), passages, rows),
        grid_spec=pltpu.PrefetchScalarGridSpec(
            num_scalar_prefetch=1,
            grid=(1,),
            in_specs=[anywhere] * (count + len(pieces))
            + [pl.BlockSpec((lines, 128), lambda i, v: (0, 0))],
            out_specs=pl.BlockSpec((lines, terms), lambda i, v: (0, 0)),
            scratch_shapes=[
                pltpu.VMEM((owners, count // owners * passages * rows, width), jnp.bfloat16),
                pltpu.VMEM((terms, width), jnp.bfloat16),
                pltpu.VMEM((owners * (terms // tile), passages, tile), jnp.float32),
                pltpu.SemaphoreType.DMA((count,)),
                pltpu.SemaphoreType.DMA((len(pieces) + terms // tile,)),
            ],
        ),
        out_shape=jax.ShapeDtypeStruct((lines, terms), jnp.bfloat16),
        cost_estimate=pl.CostEstimate(
            flops=2 * count * passages * rows * width * terms,
            bytes_accessed=2 * width * (count * passages * rows + terms),
            transcendentals=count * passages * terms * 8,
        ),
        compiler_params=pltpu.CompilerParams(vmem_limit_bytes=40 << 20),
    )(valid, *blocks, *pieces, lens_wide)


def steps(size, toward):
    return [
        (i * CORES + c, ((i + (toward if c == 0 else -toward)) % size) * CORES + c)
        for i in range(size)
        for c in range(CORES)
    ]


def swap_cores(a):
    return lax.ppermute(a, "c", [(0, 1), (1, 0)])


def hop(a, axis, toward):
    return lax.ppermute(a, (axis, "c"), steps(lax.axis_size(axis), toward))


def ring4(a, axis):
    ahead, behind = hop(a, axis, 1), hop(a, axis, -1)
    return [a, ahead, behind, hop(ahead, axis, 1)]


SHIFTS4 = (0, -1, 1, -2)
SHIFTS8 = (0, -1, 1, -2, 2, -3, 3, -4)


def placed(pooled, tile, tiles):
    onehot = (tile[:, None] == jnp.arange(tiles)[None, :]).astype(jnp.bfloat16)
    return jnp.einsum(
        "prk,rt->ptk",
        pooled.reshape(pooled.shape[0], tile.shape[0], -1),
        onehot,
        preferred_element_type=jnp.float32,
    ).astype(jnp.bfloat16)


def after(value, *others):
    return lax.optimization_barrier((value,) + others)[0]


def local(hidden, w_vocab, lengths, query_terms, tile_routes):
    groups = lax.axis_size("y")
    members = lax.axis_size("x") * lax.axis_size("z") * CORES
    docs = ("x", "z", "c")
    local_count, rows, _ = hidden.shape
    y, core = lax.axis_index("y"), lax.axis_index("c")

    at_x, at_z = lax.axis_index("x"), lax.axis_index("z")
    sign = 1 - 2 * core
    first_x, first_z = w_vocab[:ALONG_X_FIRST], w_vocab[ALONG_X_FIRST:]
    p1, s1 = hop(first_z, "z", 1), hop(first_z, "z", -1)
    line = jnp.concatenate(ring4(first_x, "x"))
    by_line = lax.all_gather(after(line, p1, s1), "z", axis=0, tiled=True)
    by_line = pltpu.with_memory_space_constraint(by_line, pltpu.HBM)
    own = ring4(hidden, "y")
    other = [swap_cores(a) for a in own]
    p2 = hop(p1, "z", 1)
    near = ring4(jnp.concatenate([first_z, p1, s1, p2]), "x")
    s2, p3 = hop(s1, "z", -1), hop(p2, "z", 1)
    s3, p4 = hop(s2, "z", -1), hop(after(p3, own[1], own[2]), "z", 1)
    far = ring4(after(jnp.concatenate([s2, p3, s3, p4]), near[1], near[2]), "x")
    tile_routes = after(tile_routes, far[2])

    lens_pair = jnp.stack([lengths, swap_cores(lengths)])
    shifts = sign * jnp.array(SHIFTS4, jnp.int32)
    places = jnp.stack([(y + shifts) % groups, (y - shifts) % groups])
    valid = jnp.clip(lens_pair[:, None, :] - places[:, :, None] * rows, 0, rows).reshape(-1)
    blocks_in = [a.reshape(local_count * rows, -1) for a in own + other]

    lens_flat = lens_pair.reshape(-1).astype(jnp.float32)
    lens_wide = jnp.broadcast_to(lens_flat[:, None], (lens_flat.shape[0], 128))
    depth = lax.axis_size("z")
    tiles_x = (at_x + shifts) % lax.axis_size("x") * depth
    around = sign * jnp.array(SHIFTS8, jnp.int32)
    tiles_z = (at_z + around) % depth
    half = len(SHIFTS8) // 2
    line_tiles = (jnp.arange(depth)[:, None] + tiles_x[None, :]).reshape(-1)
    near_tiles = (tiles_x[:, None] + tiles_z[None, :half]).reshape(-1)
    far_tiles = (tiles_x[:, None] + tiles_z[None, half:]).reshape(-1)
    term_count = query_terms.shape[1]
    tile_count = term_count // 128
    most = pooled_terms(blocks_in, valid, lens_wide, near + [by_line], rows)
    from_near, from_line = jnp.split(most, [4 * near[0].shape[0]], axis=1)
    from_far = pooled_terms(blocks_in, valid, lens_wide, far, rows)
    from_line = placed(from_line, line_tiles, tile_count)
    from_both = placed(
        jnp.concatenate([from_near, from_far], axis=1),
        jnp.concatenate([near_tiles, far_tiles]),
        tile_count,
    )
    pooled = jnp.concatenate([from_line, from_both], axis=2)
    mine = pooled[:local_count, :, None]
    theirs = swap_cores(pooled[local_count:])[:, :, None]
    blocks = jnp.where(
        core == 0,
        jnp.concatenate([mine, theirs], axis=2),
        jnp.concatenate([theirs, mine], axis=2),
    ).reshape(local_count, tile_count, 128)
    doc_terms = blocks.reshape(local_count, term_count)

    my_routes = tile_routes[0]
    capacity = min(tile_count, 4)
    passage_total = members * local_count
    owners = lax.broadcasted_iota(jnp.int32, (1, 1, members), 2)
    is_listed = jnp.any(my_routes[:, :, None] == owners, axis=1)
    earlier = lax.broadcasted_iota(jnp.int32, (tile_count, tile_count), 0)
    later = lax.broadcasted_iota(jnp.int32, (tile_count, tile_count), 1)
    slot_index = (
        lax.dot_general(
            (earlier <= later).astype(jnp.bfloat16),
            is_listed.astype(jnp.bfloat16),
            (((0,), (0,)), ((), ())),
            preferred_element_type=jnp.float32,
        ).astype(jnp.int32)
        - 1
    )
    slot_ids = lax.broadcasted_iota(jnp.int32, (1, capacity, 1), 1)
    selector = (is_listed.T[:, None, :] & (slot_index.T[:, None, :] == slot_ids)).astype(
        jnp.bfloat16
    )
    lane = lax.broadcasted_iota(jnp.int32, (1, 1, 128), 2)
    numbers = jnp.where(
        lane == 0, lax.broadcasted_iota(jnp.int32, (1, tile_count, 128), 1), 0
    ).astype(jnp.bfloat16)
    outgoing = jnp.einsum(
        "oct,ptk->ocpk",
        selector,
        jnp.concatenate([blocks, numbers], axis=0),
        preferred_element_type=jnp.float32,
    )
    line_at = lax.broadcasted_iota(jnp.int32, (local_count + 1, 128), 0)
    lane_at = lax.broadcasted_iota(jnp.int32, (local_count + 1, 128), 1)
    lens_line = jnp.zeros((local_count + 1, 128), jnp.float32)
    for p in range(local_count):
        lens_line = jnp.where(
            (line_at == local_count) & (lane_at == p + 1), lengths[p].astype(jnp.float32), lens_line
        )
    outgoing = (outgoing + lens_line).astype(jnp.bfloat16)
    arrived = lax.all_to_all(outgoing, docs, split_axis=0, concat_axis=0, tiled=True)
    notes = arrived[:, :, local_count, :].astype(jnp.float32)
    lens_in = notes[:, 0, 1 : local_count + 1]
    average = jnp.sum(lens_in) / passage_total
    denominator = saturate * (1.0 - length_slope + length_slope * lens_in / average)
    weight = arrived[:, :, :local_count, :].astype(jnp.float32)
    scaled = (
        weight * (saturate + 1.0) / (weight + denominator[:, None, :, None])
    ).astype(jnp.bfloat16)
    tile_ids = lax.broadcasted_iota(jnp.float32, (1, 1, tile_count), 2)
    placing = (notes[:, :, :1] == tile_ids).astype(jnp.bfloat16)
    masked = jnp.einsum(
        "bct,bcpk->bptk", placing, scaled, preferred_element_type=jnp.float32
    ).astype(jnp.bfloat16)
    masked = masked.reshape(passage_total, term_count)
    partial_value = lax.dot_general(
        masked, query_terms, (((1,), (1,)), ((), ())), preferred_element_type=jnp.float32
    )
    share = passage_total // groups
    parts = [
        lax.dynamic_slice_in_dim(partial_value, (y ^ k) * share, share, 0) for k in range(groups)
    ]
    scores = parts[0]
    for k in range(1, groups):
        scores = scores + lax.ppermute(parts[k], "y", [(i, i ^ k) for i in range(groups)])
    return doc_terms, scores.T


def solution(mesh):
    grid = Mesh(mesh.devices.reshape(4, 4, 8, CORES), ("y", "x", "z", "c"))
    docs = ("x", "z", "c")
    return jax.shard_map(
        local,
        mesh=grid,
        in_specs=(
            P(docs, "y", None),
            P(("y",) + docs, None),
            P(docs),
            P(docs, "y"),
            P(docs, "y", None),
        ),
        out_specs=(P(docs, "y"), P(docs, "y")),
        check_vma=False,
    )
```
